256 devices in a mesh: rows: 32 (over y, x, core), cols: 8 (over z).
Axes of the slice: x: 4, y: 4, z: 8, core: 2. Of those that a mesh axis runs over, the one named last changes fastest.
Arguments:
- weight: bfloat16 [49152, 12288], P('rows', 'cols'), may hold values from -6 to 6
- inverse_panel: float32 [256, 12288], P('rows', 'cols'), as said below
- keep_blocks: int32 [768, 4], P('rows'), may hold values 0 or 1
- calibration: bfloat16 [1536, 12288], P('rows', 'cols'), may hold values from -0.0546875 to 0.0546875
Outputs:
- pruned: bfloat16 [49152, 12288], P('rows', 'cols')
- next_input: bfloat16 [1536, 49152], P('cols', 'rows')
The draws below stay inside these ranges and needn't reach their ends.
Inputs may be any that keep to these rules, and one draw needn't show every extreme that they name: inverse_panel is upper triangular: entry (j, k) is zero for k < j; its diagonal lies between 1 and 3.
All inputs are finite; a program needn't handle non-finite values. No bound on the sum of `keep_blocks` on one device may be relied on, other than what follows from the above.
Results may differ from the reference program's by a relative error of at most 0.017.
Values may be sent and summed in bfloat16 or wider, within the bound.
A program may use at most 64 MiB of HBM per device.

```python
import math
import jax
import jax.numpy as jnp
from jax import lax

DIN = 12288
DOUT = 49152
TILE = 64
BLOCK = 128
WIN = 256
CAL = 1536
N_COLS = 8


def draw_inverse_panel(key, part):
    folded = jax.random.fold_in(key, 7)
    off_key, diag_key = jax.random.split(folded, 2)
    row_index = lax.broadcasted_iota(jnp.int32, (WIN, DIN), 0)
    col_index = lax.broadcasted_iota(jnp.int32, (WIN, DIN), 1)
    spread = jnp.clip(jax.random.normal(off_key, (WIN, DIN), jnp.float32), -4.0, 4.0)
    spread = spread * (1.0 / math.sqrt(WIN))
    diagonal = jax.random.uniform(diag_key, (WIN, 1), jnp.float32, 1.0, 3.0)
    upper = jnp.where(col_index > row_index, spread, jnp.float32(0.0))
    return jnp.where(col_index == row_index, diagonal, upper)


def touch_ends(entries, rng, smallest, high):
    longest = entries.shape.index(max(entries.shape))
    spots = []
    for shift in (0, 1):
        where = [jax.random.randint(jax.random.fold_in(rng, axis), (), 0, length) for axis, length in enumerate(entries.shape)]
        where[longest] = (where[longest] + shift) % entries.shape[longest]
        spots.append(tuple(where))
    return entries.at[spots[0]].set(smallest).at[spots[1]].set(high)


def levels(rng, shape, shards, low, high):
    level = 1.0
    for position, parts in shards:
        draws = jax.random.uniform(jax.random.fold_in(jax.random.fold_in(rng, 6), position), (parts,), jnp.float32, low / len(shards), high / len(shards))
        level = level * jnp.repeat(jnp.exp(draws), shape[position] // parts).reshape((-1,) + (1,) * (len(shape) - 1 - position))
    return level


def noise(stream_key, dims, scale, bound, shards=(), kind=jnp.bfloat16):
    entries = jax.random.normal(stream_key, dims, jnp.float32) * scale
    if len(shards) > 0:
        entries = levels(stream_key, dims, shards, -0.22, 0.18) * entries
    return jnp.clip(entries, min=-bound, max=bound).astype(kind)


def setup_inputs(seed: int = 0) -> dict:
    key_of = jax.random.split(jax.random.key(seed), 5)
    weight = noise(key_of[0], (DOUT, DIN), 1.0, 6.0, ((0, 32), (1, 8)))
    inverse_panel = draw_inverse_panel(jax.random.fold_in(key_of[4], 71), 0)
    keep_blocks = touch_ends((jax.random.randint(key_of[2], (DOUT // TILE, WIN // TILE), 0, 2) < 1).astype(jnp.int32), jax.random.fold_in(key_of[2], 1), 0, 1)
    calibration = noise(key_of[3], (CAL, DIN), DIN ** -0.5, 0.0546875, ((0, 32), (1, 8)))
    return dict(weight=weight, inverse_panel=inverse_panel, keep_blocks=keep_blocks, calibration=calibration)


def reference(weight, inverse_panel, keep_blocks, calibration):
    keep_full = jnp.repeat(jnp.repeat(keep_blocks.astype(jnp.float32), TILE, axis=0), TILE, axis=1)
    work = weight[:, :WIN].astype(jnp.float32)
    found = []
    for first in range(0, WIN, BLOCK):
        last = first + BLOCK
        current = work[:, first:last]
        prune_cols = 1.0 - keep_full[:, first:last]
        square = inverse_panel[first:last, first:last]

        def column(step, carry):
            current, errs = carry
            step = jnp.asarray(step).astype(jnp.int32)
            value = lax.dynamic_slice_in_dim(current, step, 1, 1)[:, 0]
            prune_now = lax.dynamic_slice_in_dim(prune_cols, step, 1, 1)[:, 0]
            pivot = lax.dynamic_slice(square, (step, step), (1, 1))[0, 0]
            error_col = prune_now * value / pivot
            factor_row = lax.dynamic_slice_in_dim(square, step, 1, 0)[0]
            current = current - error_col[:, None] * factor_row[None, :]
            errs = lax.dynamic_update_slice_in_dim(errs, error_col[:, None], step, 1)
            return current, errs

        current, errs = lax.fori_loop(0, BLOCK, column, (current, jnp.zeros_like(current)))
        if last < WIN:
            later = jnp.dot(errs, inverse_panel[first:last, last:WIN], precision=lax.Precision.HIGHEST)
            work = jnp.concatenate([work[:, :last], work[:, last:] - later], axis=1)
        found.append(errs)
    errors = jnp.concatenate(found, axis=1)
    width = DIN // N_COLS
    keep_padded = jnp.concatenate([keep_full, jnp.ones((DOUT, width - WIN), jnp.float32)], axis=1)

    def group(total, index):
        index = index.astype(jnp.int32)
        start = index * width
        piece = lax.dynamic_slice_in_dim(weight, start, width, 1).astype(jnp.float32)
        factor = lax.dynamic_slice_in_dim(inverse_panel, start, width, 1)
        scale = jnp.where(index == 0, keep_padded, jnp.float32(1.0))
        updated = piece - jnp.dot(errors, factor, precision=lax.Precision.HIGHEST)
        pruned_piece = (scale * updated).astype(jnp.bfloat16)
        inputs = lax.dynamic_slice_in_dim(calibration, start, width, 1)
        term = lax.dot_general(inputs, pruned_piece, (((1,), (1,)), ((), ())), preferred_element_type=jnp.float32)
        rounded = lax.optimization_barrier(term.astype(jnp.bfloat16))
        return total + rounded.astype(jnp.float32), pruned_piece

    total, pieces = lax.scan(group, jnp.zeros((CAL, DOUT), jnp.float32), jnp.arange(N_COLS, dtype=jnp.int32))
    pruned = jnp.transpose(pieces, (1, 0, 2)).reshape(DOUT, DIN)
    return pruned, total.astype(jnp.bfloat16)
```

```python
import jax
import jax.numpy as jnp
from jax import lax
from jax.experimental import pallas as pl
from jax.experimental.pallas import tpu as pltpu
from jax.sharding import PartitionSpec as P

TILE = 64
WIN = 256
F32 = jnp.float32
BF16 = jnp.bfloat16


def dot_exact(a, b):
    return lax.dot_general(
        a, b, (((1,), (0,)), ((), ())), precision=lax.Precision.HIGHEST, preferred_element_type=F32
    )


def invert_blocks(square):
    row = lax.broadcasted_iota(jnp.int32, (WIN, WIN), 0)
    col = lax.broadcasted_iota(jnp.int32, (WIN, WIN), 1)
    inverse = jnp.where(row == col, 1.0 / jnp.where(row == col, square, 1.0), 0.0)
    size = 1
    while size < TILE:
        corner = ((row // size) % 2 == 0) & (col // size == row // size + 1)
        inverse = inverse - dot_exact(dot_exact(inverse, jnp.where(corner, square, 0.0)), inverse)
        size *= 2
    return inverse


def solve_rows(weight, kept, inverse, coupling):
    col_tile = lax.broadcasted_iota(jnp.int32, weight.shape, 1) // TILE
    whole = dot_exact(weight, inverse)
    errors = jnp.where((col_tile == 0) & ~kept, whole, 0.0)
    for tile in range(1, WIN // TILE):
        now = whole - dot_exact(errors, coupling)
        errors = jnp.where((col_tile == tile) & ~kept, now, errors)
    return errors


def coupling_of(square, inverse):
    row = lax.broadcasted_iota(jnp.int32, (WIN, WIN), 0) // TILE
    col = lax.broadcasted_iota(jnp.int32, (WIN, WIN), 1) // TILE
    return dot_exact(jnp.where(row < col, square, 0.0), inverse)


def solve_kernel(weight_ref, square_ref, keep_ref, errors_ref):
    inverse = invert_blocks(square_ref[...])
    coupling = coupling_of(square_ref[...], inverse)
    groups = keep_ref.shape[0]
    lane_tile = lax.broadcasted_iota(jnp.int32, (groups, WIN), 1) // TILE
    kept = jnp.zeros((groups, WIN), jnp.int32)
    for tile in range(WIN // TILE):
        kept = jnp.where(lane_tile == tile, keep_ref[:, tile : tile + 1], kept)
    step = 6
    for first in range(0, groups, step):
        rows = pl.ds(first * TILE, step * TILE)
        mask = jnp.concatenate(
            [jnp.broadcast_to(kept[g : g + 1], (TILE, WIN)) for g in range(first, first + step)], axis=0
        )
        errors = solve_rows(weight_ref[rows, :].astype(F32), mask != 0, inverse, coupling)
        errors_ref[rows, :] = errors.astype(BF16)


def per_device(weight, inverse_panel, keep_blocks, calibration):
    gathered = lax.all_gather(inverse_panel.astype(BF16), "rows", axis=0, tiled=True)
    owner = lax.axis_index("cols") == 0
    square = jnp.where(owner, gathered[:, :WIN].astype(F32), jnp.eye(WIN, dtype=F32))
    local_errors = pl.pallas_call(
        solve_kernel,
        grid=(1,),
        out_shape=jax.ShapeDtypeStruct((weight.shape[0], WIN), BF16),
        in_specs=[
            pl.BlockSpec((weight.shape[0], WIN), lambda i: (0, 0)),
            pl.BlockSpec((WIN, WIN), lambda i: (0, 0)),
            pl.BlockSpec(keep_blocks.shape, lambda i: (0, 0)),
        ],
        out_specs=pl.BlockSpec((weight.shape[0], WIN), lambda i: (0, 0)),
        compiler_params=pltpu.CompilerParams(vmem_limit_bytes=40 << 20),
    )(weight, square, keep_blocks)
    errors = lax.psum(jnp.where(owner, local_errors, jnp.zeros_like(local_errors)), "cols")
    update = lax.dot_general(errors, gathered, (((1,), (0,)), ((), ())), preferred_element_type=F32)
    updated = weight.astype(F32) - update
    keep_full = jnp.repeat(jnp.repeat(keep_blocks.astype(F32), TILE, axis=0), TILE, axis=1)
    keep_padded = jnp.pad(keep_full, ((0, 0), (0, weight.shape[1] - WIN)), constant_values=1.0)
    window_scale = jnp.where(owner, keep_padded, F32(1.0))
    pruned = (updated * window_scale).astype(BF16)
    partial_terms = lax.dot_general(
        lax.all_gather(calibration, "rows", axis=0, tiled=True),
        pruned,
        (((1,), (1,)), ((), ())),
        preferred_element_type=F32,
    )
    next_input = lax.psum_scatter(partial_terms.astype(BF16), "cols", scatter_dimension=0, tiled=True)
    return (pruned, next_input)


def solution(mesh):
    in_specs = (P("rows", "cols"), P("rows", "cols"), P("rows", None), P("rows", "cols"))
    out_specs = (P("rows", "cols"), P("cols", "rows"))
    return jax.shard_map(
        per_device, mesh=mesh, in_specs=in_specs, out_specs=out_specs, check_vma=False
    )
```

```python
import functools

import jax
import jax.numpy as jnp
from jax import lax
from jax.experimental import pallas as pl
from jax.experimental.pallas import tpu as pltpu
from jax.sharding import PartitionSpec as P

TILE = 64
WIN = 256
F32 = jnp.float32
BF16 = jnp.bfloat16
MESH = pl.DeviceIdType.MESH

SIDE = 4
PLANE = 32
DEPTH = 8
TOKENS = 48
HALF = 768
BLOCK_TOKENS = 192
SUB = 256
SUBS = 3
LINK = 64
LINKS = HALF // LINK
HOP = 3
TICK0, TICK = 1.0, 0.65
ON = "gswcptr"


def dot_exact(a, b):
    return lax.dot_general(
        a, b, (((1,), (0,)), ((), ())), precision=lax.Precision.HIGHEST, preferred_element_type=F32
    )


def coupling_of(square, inverse):
    row = lax.broadcasted_iota(jnp.int32, (WIN, WIN), 0) // TILE
    col = lax.broadcasted_iota(jnp.int32, (WIN, WIN), 1) // TILE
    return dot_exact(jnp.where(row < col, square, 0.0), inverse)


def solve_rows(weight, kept, inverse, coupling):
    col_tile = lax.broadcasted_iota(jnp.int32, weight.shape, 1) // TILE
    whole = dot_exact(weight, inverse)
    errors = jnp.where((col_tile == 0) & ~kept, whole, 0.0)
    for tile in range(1, WIN // TILE):
        now = whole - dot_exact(errors, coupling)
        errors = jnp.where((col_tile == tile) & ~kept, now, errors)
    return errors


def fused_kernel(
    weight, panel, keep, calib, pruned, next_input,
    gath, w_v, window, panel_v, sq, inv_v, cpl_v, factor, kept_v, scale_v, errors_v, terms, ring,
    gsend, grecv, ssend, srecv, zsend, zrecv, wsend, wrecv, rsend, rrecv, local, psem,
):
    r, z = lax.axis_index("rows"), lax.axis_index("cols")
    core, x, y = lax.rem(r, 2), lax.rem(lax.div(r, 2), SIDE), lax.div(r, 2 * SIDE)
    near = lax.div(z, DEPTH // 2)

    def moved(a, b):
        down, right = a * core + b * (1 - core), a * (1 - core) + b * core
        return (lax.rem(y + down, SIDE) * SIDE + lax.rem(x + right, SIDE)) * 2 + core

    def onward(way):
        return lax.rem(z + 1 + way * (DEPTH - 2), DEPTH)

    other = r + 1 - 2 * core

    calib_left = pltpu.make_async_copy(calib.at[:, pl.ds(0, HALF)], gath.at[r, pl.ds(0, TOKENS)], local.at[0])
    calib_right = pltpu.make_async_copy(
        calib.at[:, pl.ds(HALF, HALF)], gath.at[r, pl.ds(TOKENS, TOKENS)], local.at[1]
    )
    panel_load = pltpu.make_async_copy(panel, panel_v, local.at[2])
    weight_load = pltpu.make_async_copy(weight, w_v, local.at[3])
    window_load = pltpu.make_async_copy(weight.at[:, pl.ds(0, WIN)], window, local.at[4])
    panel_load.start()
    calib_left.start()
    calib_right.start()

    @pl.when(z == 0)
    def _():
        window_load.start()

    weight_load.start()

    barrier = pltpu.get_barrier_semaphore()

    def greet_plane(k, carry):
        pl.semaphore_signal(barrier, inc=1, device_id=(lax.rem(r + k, PLANE), z), device_id_type=MESH)
        return carry

    def greet_column(k, carry):
        pl.semaphore_signal(barrier, inc=1, device_id=(r, lax.rem(z + k, DEPTH)), device_id_type=MESH)
        return carry

    lax.fori_loop(1, PLANE, greet_plane, 0)
    lax.fori_loop(1, DEPTH, greet_column, 0)
    panel_load.wait()

    rows8 = panel_v[...]
    gath[r, pl.ds(2 * TOKENS, 16), :] = jnp.concatenate([rows8[:, :HALF], rows8[:, HALF:]], axis=0).astype(BF16)

    @pl.when(z == 0)
    def _():
        sq[r] = panel_v[:, pl.ds(0, WIN)]

    groups = keep.shape[0]
    lane_tile = lax.broadcasted_iota(jnp.int32, (groups, WIN), 1) // TILE
    kept = jnp.zeros((groups, WIN), jnp.int32)
    for tile in range(WIN // TILE):
        kept = jnp.where(lane_tile == tile, keep[:, tile : tile + 1], kept)
    kept_v[...] = kept
    scale_v[...] = jnp.where(z == 0, kept, 1)

    calib_left.wait()
    calib_right.wait()
    pl.semaphore_wait(barrier, PLANE - 1 + DEPTH - 1)

    def square_down(k):
        return pltpu.make_async_remote_copy(
            src_ref=sq.at[r], dst_ref=sq.at[r], send_sem=zsend.at[k - 1], recv_sem=zrecv.at[0],
            device_id=(r, lax.rem(z + k, DEPTH)), device_id_type=MESH,
        )

    def square_across(k, slot):
        return pltpu.make_async_remote_copy(
            src_ref=sq.at[slot], dst_ref=sq.at[slot], send_sem=ssend.at[k - 1], recv_sem=srecv.at[slot],
            device_id=(lax.rem(r + k, PLANE), z), device_id_type=MESH,
        )

    def shard(slot, sem, to):
        return pltpu.make_async_remote_copy(
            src_ref=gath.at[slot], dst_ref=gath.at[slot], send_sem=gsend.at[sem], recv_sem=grecv.at[slot],
            device_id=(to, z), device_id_type=MESH,
        )

    def link(way, i):
        rows = pl.ds(pl.multiple_of(way * HALF + i * LINK, LINK), LINK)
        return pltpu.make_async_remote_copy(
            src_ref=window.at[rows], dst_ref=window.at[rows], send_sem=wsend.at[way, i], recv_sem=wrecv.at[way, i],
            device_id=(r, onward(way)), device_id_type=MESH,
        )

    def piece(way, sub, step):
        return pltpu.make_async_remote_copy(
            src_ref=ring.at[way, sub, step], dst_ref=ring.at[way, sub, step + 1],
            send_sem=rsend.at[way, sub, step], recv_sem=rrecv.at[way, sub, step],
            device_id=(r, onward(way)), device_id_type=MESH,
        )

    def block_of(way, step):
        ahead = lax.rem(z + DEPTH - 1 - step + way * (2 * step + 2 - DEPTH), DEPTH)
        return pl.multiple_of(ahead * BLOCK_TOKENS, BLOCK_TOKENS)

    handed = []

    def give(slot, to):
        handed.append(None)
        shard(slot, len(handed) - 1, to).start()

    def first_sends():
        @pl.when(z == 0)
        def _():
            for k in range(1, DEPTH):
                square_down(k).start()
            window_load.wait()

            def send(i, carry):
                link(0, i).start()
                link(1, i).start()
                return carry

            lax.fori_loop(0, LINKS, send, 0)

        for k in (1, 3):
            give(r, moved(k, 0))
            give(r, moved(0, k))
        give(r, moved(2, 0))
        give(r, other)

    def squares_on():
        @pl.when(z != 0)
        def _():
            square_down(1).wait_recv()

        def send(k, carry):
            square_across(k, r).start()
            return carry

        lax.fori_loop(1, PLANE, send, 0)

    def take_squares():
        def take(k, carry):
            square_across(k, lax.rem(r + PLANE - k, PLANE)).wait_recv()
            return carry

        lax.fori_loop(1, PLANE, take, 0)

    def along_first(j):
        slot = moved(SIDE - j, 0)
        shard(slot, 0, other).wait_recv()
        for k in (1, 3):
            give(slot, moved(0, k))
        give(slot, other)

    def along_second(j, k):
        slot = moved(SIDE - j, SIDE - k)
        shard(slot, 0, other).wait_recv()
        if (k == 1 and j in (0, 1)) or (k == 3 and j in (2, 3)):
            give(slot, moved(0, k))
        give(slot, other)

    def take_other():
        def take(q, carry):
            shard(2 * q + 1 - core, 0, other).wait_recv()
            return carry

        lax.fori_loop(0, PLANE // 2, take, 0)

    def tick(n):
        for way in range(2):
            hops = z if way == 0 else DEPTH - z
            i = n - HOP * hops

            @pl.when((z != 0) & (i >= 0) & (i < LINKS))
            def _(way=way, i=i, hops=hops):
                link(way, i).wait_recv()

                @pl.when(hops != DEPTH - 1)
                def _():
                    link(way, i).start()

    def invert_start():
        row = lax.broadcasted_iota(jnp.int32, (WIN, WIN), 0)
        col = lax.broadcasted_iota(jnp.int32, (WIN, WIN), 1)
        square = sq[...].reshape(WIN, WIN)
        inv_v[...] = jnp.where(row == col, 1.0 / jnp.where(row == col, square, 1.0), 0.0)

    def invert_level(size):
        row = lax.broadcasted_iota(jnp.int32, (WIN, WIN), 0)
        col = lax.broadcasted_iota(jnp.int32, (WIN, WIN), 1)
        square = sq[...].reshape(WIN, WIN)
        inverse = inv_v[...]
        corner = ((row // size) % 2 == 0) & (col // size == row // size + 1)
        inv_v[...] = inverse - dot_exact(dot_exact(inverse, jnp.where(corner, square, 0.0)), inverse)

    def couple():
        cpl_v[...] = coupling_of(sq[...].reshape(WIN, WIN), inv_v[...])

    def expand(ref, first):
        group = lax.div(first, TILE)
        return jnp.concatenate(
            [jnp.broadcast_to(ref[pl.ds(group + g, 1), :], (TILE, WIN)) for g in range(SUB // TILE)], axis=0
        )

    def start_of(way, sub):
        return pl.multiple_of(way * HALF + sub * SUB, SUB)

    def solve(way, sub):
        first = start_of(way, sub)
        rows = pl.ds(first, SUB)
        errors = solve_rows(window[rows, :].astype(F32), expand(kept_v, first) != 0, inv_v[...], cpl_v[...])
        errors_v[rows, :] = errors.astype(BF16)

    def make_factor():
        both = gath[:, pl.ds(2 * TOKENS, 16), :].astype(F32)
        factor[:, pl.ds(0, HALF)] = both[:, 0:8].reshape(WIN, HALF).astype(BF16)
        factor[:, pl.ds(HALF, HALF)] = both[:, 8:16].reshape(WIN, HALF).astype(BF16)

    def prune(way, sub):
        first = start_of(way, sub)
        rows = pl.ds(first, SUB)
        updated = w_v[rows, :].astype(F32) - jnp.dot(errors_v[rows, :], factor[...], preferred_element_type=F32)
        in_window = jnp.where(expand(scale_v, first) != 0, updated[:, :WIN], 0.0)
        w_v[rows, :] = jnp.concatenate([in_window, updated[:, WIN:]], axis=1).astype(BF16)
        pltpu.make_async_copy(w_v.at[rows], pruned.at[rows], psem.at[way * SUBS + sub]).start()

    def multiply(way, sub):
        rows = pl.ds(start_of(way, sub), SUB)
        new_left, new_right = w_v[rows, pl.ds(0, HALF)], w_v[rows, pl.ds(HALF, HALF)]

        def term(t, carry):
            sent = gath[pl.ds(t * 16, 16), pl.ds(0, 2 * TOKENS), :]
            left = sent[:, :TOKENS].reshape(16 * TOKENS, HALF)
            right = sent[:, TOKENS:].reshape(16 * TOKENS, HALF)
            dims = (((1,), (1,)), ((), ()))
            total = lax.dot_general(left, new_left, dims, preferred_element_type=F32)
            total += lax.dot_general(right, new_right, dims, preferred_element_type=F32)
            at_rows = pl.ds(pl.multiple_of(t * 16 * TOKENS, 16 * TOKENS), 16 * TOKENS)
            terms[way * SUBS + sub, at_rows, :] = total.astype(BF16)
            return carry

        lax.fori_loop(0, 2, term, 0)

    def launch(way, sub):
        ring[way, sub, 0] = terms[way * SUBS + sub, pl.ds(block_of(way, 0), BLOCK_TOKENS), :]
        piece(way, sub, 0).start()

    plan = []

    def do(when, tag, f, *a):
        if tag in ON:
            plan.append((when, len(plan), f, a))

    do(0.0, "g", first_sends)
    do(2.0, "s", squares_on)
    for j, when in ((1, 3.0), (3, 3.2), (2, 5.0)):
        do(when, "g", along_first, j)
    for j, when in ((0, 3.5), (1, 6.0), (3, 7.0), (2, 9.0)):
        do(when, "g", along_second, j, 1)
        do(when + 0.1, "g", along_second, j, 3)
        do(when + 4.0, "g", along_second, j, 2)
    do(14.0, "g", take_other)
    for n in range(HOP, HOP * (DEPTH - 1) + LINKS):
        do(TICK0 + TICK * n, "w", tick, n)
    do(6.1, "s", take_squares)
    do(6.2, "c", invert_start)
    for level in range(6):
        do(6.3 + 0.7 * level, "c", invert_level, 2**level)
    do(10.5, "c", couple)
    for sub in range(SUBS):
        do(TICK0 + TICK * (HOP * 4 + (SUB // LINK) * (sub + 1) - 1) + 0.01, "c", solve, near, sub)
    at_far = [TICK0 + TICK * (HOP * 7 + (SUB // LINK) * (sub + 1) - 1) + 0.01 for sub in range(SUBS)]
    do(14.1, "p", weight_load.wait)
    do(14.2, "p", make_factor)
    for sub in range(SUBS):
        for way, when in ((near, max(14.3, at_far[sub] - 1.0)), (1 - near, at_far[sub] + 0.1)):
            if way is not near:
                do(when, "c", solve, way, sub)
            do(when, "p", prune, way, sub)
            do(when, "t", multiply, way, sub)
            do(when, "r", launch, way, sub)
    for _, _, f, a in sorted(plan, key=lambda e: e[:2]):
        f(*a)
    if "p" not in ON:
        weight_load.wait()

    for step in range(1, DEPTH) if "r" in ON else ():
        for sub in range(SUBS):
            for way in (near, 1 - near):
                piece(way, sub, step - 1).wait_recv()
                mine = terms[way * SUBS + sub, pl.ds(block_of(way, step), BLOCK_TOKENS), :].astype(F32)
                total = (ring[way, sub, step].astype(F32) + mine).astype(BF16)
                if step < DEPTH - 1:
                    ring[way, sub, step] = total
                    piece(way, sub, step).start()
                else:
                    next_input[:, pl.ds(start_of(way, sub), SUB)] = total

    if "g" in ON:

        @pl.when(z == 0)
        def _():
            for k in range(1, DEPTH):
                square_down(k).wait_send()

    def sent_square(k, carry):
        square_across(k, r).wait_send()
        return carry

    def sent_shard(s, carry):
        shard(r, s, other).wait_send()
        return carry

    def sent_link(i, carry):
        for way in range(2):

            @pl.when(z != (DEPTH - 1 if way == 0 else 1))
            def _(way=way):
                link(way, i).wait_send()

        return carry

    def sent_piece(step, carry):
        for way in range(2):
            for sub in range(SUBS):
                piece(way, sub, step).wait_send()
        return carry

    lax.fori_loop(1, PLANE if "s" in ON else 1, sent_square, 0)
    lax.fori_loop(0, len(handed), sent_shard, 0)
    lax.fori_loop(0, LINKS if "w" in ON else 0, sent_link, 0)
    lax.fori_loop(0, DEPTH - 1 if "r" in ON else 0, sent_piece, 0)
    for i in range(2 * SUBS if "p" in ON else 0):
        rows = pl.ds(i * SUB, SUB)
        pltpu.make_async_copy(w_v.at[rows], pruned.at[rows], psem.at[i]).wait()


def per_device(weight, inverse_panel, keep_blocks, calibration):
    rows, columns = weight.shape
    anywhere = pl.BlockSpec(memory_space=pl.ANY)
    vmem = pl.BlockSpec(memory_space=pltpu.VMEM)
    dma = pltpu.SemaphoreType.DMA
    return pl.pallas_call(
        fused_kernel,
        out_shape=(
            jax.ShapeDtypeStruct((rows, columns), BF16),
            jax.ShapeDtypeStruct((BLOCK_TOKENS, rows), BF16),
        ),
        in_specs=[anywhere, anywhere, vmem, anywhere],
        out_specs=(anywhere, vmem),
        scratch_shapes=[
            pltpu.VMEM((PLANE, 2 * TOKENS + 16, HALF), BF16),
            pltpu.VMEM((rows, columns), BF16),
            pltpu.VMEM((rows, WIN), BF16),
            pltpu.VMEM((8, columns), F32),
            pltpu.VMEM((PLANE, 8, WIN), F32),
            pltpu.VMEM((WIN, WIN), F32),
            pltpu.VMEM((WIN, WIN), F32),
            pltpu.VMEM((WIN, columns), BF16),
            pltpu.VMEM((rows // TILE, WIN), jnp.int32),
            pltpu.VMEM((rows // TILE, WIN), jnp.int32),
            pltpu.VMEM((rows, WIN), BF16),
            pltpu.VMEM((2 * SUBS, PLANE * TOKENS, SUB), BF16),
            pltpu.VMEM((2, SUBS, DEPTH, BLOCK_TOKENS, SUB), BF16),
            dma((32,)), dma((PLANE,)), dma((31,)), dma((PLANE,)), dma((7,)), dma((1,)),
            dma((2, LINKS)), dma((2, LINKS)), dma((2, SUBS, DEPTH - 1)), dma((2, SUBS, DEPTH - 1)),
            dma((5,)), dma((2 * SUBS,)),
        ],
        compiler_params=pltpu.CompilerParams(
            collective_id=0, has_side_effects=True, vmem_limit_bytes=56 << 20
        ),
    )(weight, inverse_panel, keep_blocks, calibration)


def solution(mesh):
    in_specs = (P("rows", "cols"), P("rows", "cols"), P("rows", None), P("rows", "cols"))
    out_specs = (P("rows", "cols"), P("cols", "rows"))
    return jax.shard_map(
        per_device, mesh=mesh, in_specs=in_specs, out_specs=out_specs, check_vma=False
    )
```
